32 devices in a mesh: dp: 8 (over y, x, core), fsdp: 4 (over z).
Axes of the slice: x: 2, y: 2, z: 4, core: 2. Of those that a mesh axis runs over, the one named last changes fastest.
Arguments:
- tokens: bfloat16 [2, 32, 256, 1536], P(None, ('dp', 'fsdp')), may hold values from -6 to 6
- norm_gain: bfloat16 [1536], P(('dp', 'fsdp')), may hold values from 0.5 to 1.5
- main_projection_weight: bfloat16 [1536, 6400], P(('dp', 'fsdp')), may hold values from -0.15625 to 0.15625
- step_size_weight: bfloat16 [1536, 48], P(('dp', 'fsdp')), may hold values from -0.15625 to 0.15625
- conv_weight: bfloat16 [4, 3328], P(None, ('dp', 'fsdp')), may hold values from -3 to 3
- conv_bias: bfloat16 [3328], P(('dp', 'fsdp')), may hold values from -3 to 3
- a_log: float32 [48], replicated, may hold values from 0 to 2.77
- d_skip: float32 [48], replicated, may hold values from 0.5 to 1.5
- dt_bias: float32 [48], replicated, may hold values from -6.9 to -2.3
- norm2_gain: bfloat16 [3072], P(('dp', 'fsdp')), may hold values from 0.5 to 1.5
- output_projection_weight: bfloat16 [3072, 1536], P(('dp', 'fsdp')), may hold values from -0.109375 to 0.109375
- cotangent: bfloat16 [2, 32, 256, 1536], P(None, ('dp', 'fsdp')), may hold values from -6 to 6
Outputs:
- block_out: bfloat16 [2, 32, 256, 1536], P(None, ('dp', 'fsdp'))
- tokens_grad: float32 [2, 32, 256, 1536], P(None, ('dp', 'fsdp'))
- norm_gain_grad: float32 [1536], P(('dp', 'fsdp'))
- w_main_grad: float32 [1536, 6400], P(('dp', 'fsdp'))
- w_dt_grad: float32 [1536, 48], P(('dp', 'fsdp'))
- conv_weight_grad: float32 [4, 3328], P(None, ('dp', 'fsdp'))
- conv_bias_grad: float32 [3328], P(('dp', 'fsdp'))
- a_log_grad: float32 [48], replicated
- d_skip_grad: float32 [48], replicated
- dt_bias_grad: float32 [48], replicated
- norm2_gain_grad: float32 [3072], P(('dp', 'fsdp'))
- w_out_grad: float32 [3072, 1536], P(('dp', 'fsdp'))
The draws below stay inside these ranges and needn't reach their ends.
All inputs are finite; a program needn't handle non-finite values.
Results may differ from the reference program's by a relative error of at most 0.0076.
Values may be sent and summed in bfloat16 or wider, within the bound.
No kernel may reach another device: no remote copies, remote signals or barrier semaphores. Data moves between devices by JAX's collectives and lax.ppermute only.
A program may use at most 256 MiB of HBM per device.

```python
import math
import jax
import jax.numpy as jnp
from jax import lax

D = 1536
DI = 3072
HEADS = 48
CONV = 4
SPAN = 256
L = 256
MB = 2
BATCH = 32
CH = 3328
PROJ = 6400


def steps_of(rng, shape, split, least, high):
    level, own = 1.0, jax.random.fold_in(rng, 6)
    for dim, blocks in split:
        heights = jnp.exp(jax.random.uniform(jax.random.fold_in(own, dim), (blocks,), jnp.float32, least / len(split), high / len(split)))
        level = level * jnp.repeat(heights, shape[dim] // blocks).reshape([-1 if axis == dim else 1 for axis in range(len(shape))])
    return level


def normal_values(stream_key, shape, deviation, limit, split=(), kind=jnp.bfloat16):
    values = jax.random.normal(stream_key, shape, jnp.float32) * deviation
    if len(split) > 0:
        values = steps_of(stream_key, shape, split, -0.22, 0.18) * values
    return jnp.clip(values, min=-limit, max=limit).astype(kind)


def setup_inputs(seed: int = 0) -> dict:
    splits = jax.random.split(jax.random.key(seed), 13)
    return {
        "tokens": normal_values(splits[0], (MB, BATCH, L, D), 1.0, 6.0, ((1, 32),)),
        "norm_gain": jnp.clip(1.0 + 0.1 * jax.random.normal(splits[1], (D,), jnp.float32), 0.5, 1.5).astype(jnp.bfloat16),
        "main_projection_weight": normal_values(splits[2], (D, PROJ), D ** -0.5, 0.15625, ((0, 32),)),
        "step_size_weight": normal_values(splits[3], (D, HEADS), D ** -0.5, 0.15625, ((0, 32),)),
        "conv_weight": normal_values(splits[4], (CONV, CH), CONV ** -0.5, 3.0, ((1, 32),)),
        "conv_bias": normal_values(splits[5], (CH,), 0.5, 3.0, ((0, 32),)),
        "a_log": jnp.clip(jax.random.uniform(splits[6], (HEADS,), jnp.float32, 0.0, 2.77), 0.0, 2.77),
        "d_skip": jnp.clip(jax.random.uniform(splits[7], (HEADS,), jnp.float32, 0.5, 1.5), 0.5, 1.5),
        "dt_bias": jnp.clip(jax.random.uniform(splits[8], (HEADS,), jnp.float32, -6.9, -2.3), -6.9, -2.3),
        "norm2_gain": jnp.clip(1.0 + 0.1 * jax.random.normal(splits[9], (DI,), jnp.float32), 0.5, 1.5).astype(jnp.bfloat16),
        "output_projection_weight": normal_values(splits[10], (DI, D), DI ** -0.5, 0.109375, ((0, 32),)),
        "cotangent": normal_values(splits[11], (MB, BATCH, L, D), 1.0, 6.0, ((1, 32),)),
    }


@jax.custom_vjp
def low(v):
    return lax.optimization_barrier(v.astype(jnp.bfloat16)).astype(jnp.float32)

@jax.custom_vjp
def reduced_backward_copy(v):
    return v

def low_keep(v):
    return (low(v), None)

def low_pass(kept, grad):
    return (grad,)

def back_keep(v):
    return (v, None)

def back_low(kept, grad):
    return (low(grad),)
low.defvjp(low_keep, low_pass)
reduced_backward_copy.defvjp(back_keep, back_low)
epsilon = 1e-05
exact_precision = lax.Precision.HIGHEST

def mixer_forward(projected_input, step_size_input, conv_weight, conv_bias, norm2_gain, a_log, d_skip, dt_bias):
    inner_width = norm2_gain.shape[0]
    head_count = a_log.shape[0]
    head_size = inner_width // head_count
    kernel_width = conv_weight.shape[0]
    state_dim = (conv_weight.shape[1] - inner_width) // 2
    batch_seqs = projected_input.shape[0]
    seq_len = projected_input.shape[1]
    gate_part = projected_input[..., :inner_width]
    conv_in = projected_input[..., inner_width:]
    padded = jnp.pad(conv_in, ((0, 0), (kernel_width - 1, 0), (0, 0)))
    conv_pre = conv_bias + conv_weight[0] * padded[:, 0:seq_len]
    for offset in range(1, kernel_width):
        conv_pre = conv_pre + conv_weight[offset] * padded[:, offset:offset + seq_len]
    conv_out = jax.nn.silu(conv_pre)
    head_values = conv_out[..., :inner_width].reshape(batch_seqs, seq_len, head_count, head_size)
    b_rows = conv_out[..., inner_width:inner_width + state_dim]
    c_rows = conv_out[..., inner_width + state_dim:]
    step_sizes = jax.nn.softplus(step_size_input + dt_bias)
    decay_rate = -jnp.exp(a_log)
    blocks = seq_len // SPAN

    def split_blocks(array_in):
        return jnp.swapaxes(array_in.reshape((batch_seqs, blocks, SPAN) + array_in.shape[2:]), 0, 1)
    lower_mask = lax.broadcasted_iota(jnp.int32, (SPAN, SPAN), 0) >= lax.broadcasted_iota(jnp.int32, (SPAN, SPAN), 1)

    def block_step(state_in, block_inputs):
        values_block, b_block, c_block, dt_block = block_inputs
        decay_log = jnp.cumsum(dt_block * decay_rate, axis=1)
        log_heads = jnp.swapaxes(decay_log, 1, 2)
        dt_heads = jnp.swapaxes(dt_block, 1, 2)
        log_gaps = log_heads[..., :, None] - log_heads[..., None, :]
        decay_mat = jnp.exp(jnp.where(lower_mask, log_gaps, 0.0)) * lower_mask.astype(log_gaps.dtype)
        scores = jnp.einsum('sin,sjn->sij', c_block, b_block, precision=exact_precision)
        mixing = scores[:, None] * decay_mat * dt_heads[:, :, None, :]
        inside = jnp.einsum('shij,sjhp->sihp', mixing, values_block, precision=exact_precision)
        carried = jnp.einsum('sin,shpn->sihp', c_block, state_in, precision=exact_precision) * jnp.exp(decay_log)[..., None]
        tail_weight = jnp.exp(log_heads[..., -1:] - log_heads) * dt_heads
        weighted = values_block * jnp.swapaxes(tail_weight, 1, 2)[..., None]
        new_state = state_in * jnp.exp(log_heads[..., -1])[..., None, None] + jnp.einsum('sjhp,sjn->shpn', weighted, b_block, precision=exact_precision)
        output = inside + carried + d_skip[:, None] * values_block
        return (new_state, output)
    zero_state = jnp.zeros((batch_seqs, head_count, head_size, state_dim), jnp.float32)
    _, outputs = lax.scan(jax.checkpoint(block_step), zero_state, (split_blocks(head_values), split_blocks(b_rows), split_blocks(c_rows), split_blocks(step_sizes)))
    ssd_out = jnp.swapaxes(outputs, 0, 1).reshape(batch_seqs, seq_len, inner_width)
    mixed = ssd_out * jax.nn.silu(gate_part)
    return mixed * lax.rsqrt(lax.optimization_barrier(jnp.mean(mixed * mixed, axis=-1, keepdims=True)) + epsilon) * norm2_gain

def block_forward(token_batch_input, norm_gain, main_projection_weight, step_size_weight, conv_weight, conv_bias, a_log, d_skip, dt_bias, norm2_gain, output_projection_weight):
    inv_rms = lax.rsqrt(lax.optimization_barrier(jnp.mean(token_batch_input * token_batch_input, axis=-1, keepdims=True)) + epsilon)
    normalized_input = low(token_batch_input * inv_rms * norm_gain)
    projected_input = reduced_backward_copy(jnp.einsum('wkc,cb->wkb', normalized_input, main_projection_weight, precision=exact_precision))
    step_size_input = reduced_backward_copy(jnp.einsum('rvf,fz->rvz', normalized_input, step_size_weight, precision=exact_precision))
    gated_result = low(mixer_forward(projected_input, step_size_input, conv_weight, conv_bias, norm2_gain, a_log, d_skip, dt_bias))
    return token_batch_input + jnp.einsum('azm,mq->azq', gated_result, output_projection_weight, precision=exact_precision)

def reference(tokens, norm_gain, main_projection_weight, step_size_weight, conv_weight, conv_bias, a_log, d_skip, dt_bias, norm2_gain, output_projection_weight, cotangent):
    seq_total = MB * BATCH
    group_size = math.gcd(seq_total, max(1, 4096 // L))
    group_count = seq_total // group_size
    grouped_in = tokens.astype(jnp.float32).reshape(group_count, group_size, L, D)
    grouped_cot = cotangent.astype(jnp.float32).reshape(group_count, group_size, L, D)
    params = (norm_gain.astype(jnp.float32), main_projection_weight.astype(jnp.float32), step_size_weight.astype(jnp.float32), conv_weight.astype(jnp.float32), conv_bias.astype(jnp.float32), a_log.astype(jnp.float32), d_skip.astype(jnp.float32), dt_bias.astype(jnp.float32), norm2_gain.astype(jnp.float32), output_projection_weight.astype(jnp.float32))

    def one_group(totals, group_inputs):
        seq_in, seq_cot = group_inputs
        result, pullback = jax.vjp(block_forward, seq_in, *params)
        grads = pullback(seq_cot)
        new_totals = jax.tree.map(jnp.add, totals, tuple(grads[1:]))
        return (new_totals, (result.astype(jnp.bfloat16), grads[0]))
    zero_totals = tuple((jnp.zeros_like(param) for param in params))
    totals, (results, input_grads) = lax.scan(one_group, zero_totals, (grouped_in, grouped_cot))
    block_out = results.reshape(MB, BATCH, L, D)
    tokens_grad = input_grads.reshape(MB, BATCH, L, D)
    return (block_out, tokens_grad, totals[0], totals[1], totals[2], totals[3], totals[4], totals[5], totals[6], totals[7], totals[8], totals[9])
```

```python
import functools

import jax
import jax.numpy as jnp
from jax import lax
from jax.experimental import pallas as pl
from jax.experimental.pallas import tpu as pltpu
from jax.sharding import Mesh
from jax.sharding import PartitionSpec as P


epsilon = 1e-05
f32 = jnp.float32
bf16 = jnp.bfloat16
LANES = 128
ALL_AXES = ("y", "x", "core", "z")


def swap_core(array):
    return lax.ppermute(array, "core", [(0, 1), (1, 0)])


def line_gather(array, axis, count, place):
    index = lax.axis_index(axis)
    if count == 1:
        return jnp.expand_dims(array, place)
    if count == 2:
        other = lax.ppermute(array, axis, [(0, 1), (1, 0)])
        first = index == 0
        return jnp.stack(
            [jnp.where(first, array, other), jnp.where(first, other, array)], axis=place
        )
    to_right = [(i, i + 1) for i in range(count - 1)]
    to_left = [(i + 1, i) for i in range(count - 1)]
    from_left, from_right = [array], [array]
    for _ in range(count - 1):
        from_left.append(lax.ppermute(from_left[-1], axis, to_right))
        from_right.append(lax.ppermute(from_right[-1], axis, to_left))
    shape = array.shape[:place] + (count,) + array.shape[place:]
    result = jnp.zeros(shape, array.dtype)
    for step in range(count):
        if step == 0:
            block = array
        else:
            block = jnp.where(index >= step, from_left[step], from_right[count - step])
        slot = lax.rem(index - step + count, count)
        result = lax.dynamic_update_slice_in_dim(
            result, jnp.expand_dims(block, place), slot, axis=place
        )
    return result


def add_parts(*parts):
    total = parts[0].astype(f32)
    for part in parts[1:]:
        total = total + part.astype(f32)
    return total.astype(parts[0].dtype)


def line_scatter(array, axis, count, place):
    index = lax.axis_index(axis)

    def entry(which):
        return lax.dynamic_index_in_dim(array, which, axis=place, keepdims=False)

    if count == 1:
        return entry(0)
    if count == 2:
        other = lax.ppermute(entry(1 - index), axis, [(0, 1), (1, 0)])
        return add_parts(entry(index), other)
    right = left = None
    for step in range(count - 1):
        for_right = entry(jnp.clip(count - 1 - step + index, 0, count - 1))
        for_left = entry(jnp.clip(step - (count - 1 - index), 0, count - 1))
        if step > 0:
            for_right = add_parts(for_right, right)
            for_left = add_parts(for_left, left)
        senders = range(min(step, count - 2) + 1)
        right = lax.ppermute(for_right, axis, [(i, i + 1) for i in senders])
        left = lax.ppermute(for_left, axis, [(count - 1 - i, count - 2 - i) for i in senders])
    return add_parts(entry(index), right, left)


def gather_chunk(shard, counts):
    ny, nx, nz = counts
    own = line_gather(shard, "z", nz, shard.ndim - 2)
    half = own.shape[-1] // 2
    one, two = own[..., :half], own[..., half:]
    one = line_gather(line_gather(one, "y", ny, 0), "x", nx, 1)
    two = line_gather(line_gather(two, "x", nx, 0), "y", ny, 0)
    return jnp.concatenate([one, two], axis=-1)


def scatter_chunk(grads, counts):
    ny, nx, nz = counts
    half = grads.shape[-1] // 2
    one, two = grads[..., :half], grads[..., half:]
    one = line_scatter(line_scatter(one, "x", nx, 1), "y", ny, 0)
    two = line_scatter(line_scatter(two, "y", ny, 0), "x", nx, 0)
    both = jnp.concatenate([one, two], axis=-1)
    return line_scatter(both, "z", nz, both.ndim - 3)


def shifted_down(values, steps):
    rows = lax.broadcasted_iota(jnp.int32, values.shape, 0)
    return jnp.where(rows >= steps, pltpu.roll(values, steps, 0), 0.0)


def shifted_up(values, steps):
    count = values.shape[0]
    rows = lax.broadcasted_iota(jnp.int32, values.shape, 0)
    return jnp.where(rows < count - steps, pltpu.roll(values, count - steps, 0), 0.0)


def running_sum(values):
    step = 1
    while step < values.shape[0]:
        values = values + shifted_down(values, step)
        step *= 2
    return values


def running_sum_back(values):
    step = 1
    while step < values.shape[0]:
        values = values + shifted_up(values, step)
        step *= 2
    return values


def conv_taps(values, width):
    return [values if k == width - 1 else shifted_down(values, width - 1 - k) for k in range(width)]


def conv_pre_of(taps, weight, bias):
    total = bias + weight[0:1, :] * taps[0]
    for k in range(1, len(taps)):
        total = total + weight[k : k + 1, :] * taps[k]
    return total


def dot32(a, b, dims):
    return lax.dot_general(
        a, b, (dims, ((), ())), precision=lax.Precision.HIGHEST, preferred_element_type=f32
    )


def dot16(a, b, dims):
    return lax.dot_general(a, b, (dims, ((), ())), preferred_element_type=f32)


def softplus(v):
    return jnp.maximum(v, 0.0) + jnp.log1p(jnp.exp(-jnp.abs(v)))


MASKED = -1e30


def prepare_steps(step_ref, head_ref, decay_cols, decay_rows, dt_scr, heads):
    dt = softplus(step_ref[...] + head_ref[0:1, :])
    dt_scr[...] = dt
    decay = running_sum(dt * head_ref[1:2, :])
    decay_rows[...] = decay.T
    for h in range(heads):
        decay_cols[h] = jnp.broadcast_to(decay[:, h : h + 1], (decay.shape[0], LANES))


def forward_kernel(
    width, heads, heads_here, head_size,
    x_ref, bc_ref, step_ref, cw_ref, cb_ref, cwbc_ref, cbbc_ref, head_ref, spread_ref, skip_ref,
    out_ref, scores, decay_cols, decay_rows, dt_scr,
):
    block = pl.program_id(1)
    span = x_ref.shape[0]
    state = bc_ref.shape[1] // 2
    half = span // 2

    @pl.when(block == 0)
    def _():
        pre = conv_pre_of(conv_taps(bc_ref[...], width), cwbc_ref[...], cbbc_ref[...])
        act = pre * jax.nn.sigmoid(pre)
        scores[...] = dot32(act[:, state:], act[:, :state], ((1,), (1,)))
        prepare_steps(step_ref, head_ref, decay_cols, decay_rows, dt_scr, heads)

    pre = conv_pre_of(conv_taps(x_ref[...], width), cw_ref[...], cb_ref[...])
    xs = pre * jax.nn.sigmoid(pre)
    weighted = (xs * dot32(dt_scr[...], spread_ref[...], ((1,), (0,)))).astype(bf16)
    lower = lax.broadcasted_iota(jnp.int32, (half, half), 0) >= lax.broadcasted_iota(
        jnp.int32, (half, half), 1
    )
    per_lane = LANES // head_size
    lane = lax.broadcasted_iota(jnp.int32, (span, LANES), 1)
    for group in range(heads_here // per_lane):
        cols = slice(group * LANES, (group + 1) * LANES)
        wide = weighted[:, cols]
        top_n, bottom_n, top_v, bottom_v = [], [], [], []
        for k in range(per_lane):
            h = block * heads_here + group * per_lane + k
            col = decay_cols[h]
            row = decay_rows[pl.ds(h, 1), :]
            gap = jnp.where(lower, col[:half, :half] - row[:, :half], MASKED)
            n00 = (scores[:half, :half] * jnp.exp(gap)).astype(bf16)
            n10 = (scores[half:, :half] * jnp.exp(col[half:, :half] - row[:, :half])).astype(bf16)
            gap = jnp.where(lower, col[half:, :half] - row[:, half:], MASKED)
            n11 = (scores[half:, half:] * jnp.exp(gap)).astype(bf16)
            masked = jnp.where(lane // head_size == k, wide, jnp.zeros_like(wide))
            top_n.append(n00)
            top_v.append(masked[:half])
            bottom_n += [n10, n11]
            bottom_v.append(masked)
        top = dot16(jnp.concatenate(top_n, 1), jnp.concatenate(top_v, 0), ((1,), (0,)))
        bottom = dot16(jnp.concatenate(bottom_n, 1), jnp.concatenate(bottom_v, 0), ((1,), (0,)))
        skip = skip_ref[:, cols]
        out_ref[:half, cols] = top + skip * xs[:half, cols]
        out_ref[half:, cols] = bottom + skip * xs[half:, cols]


def conv_back(d_pre, weight, width):
    total = weight[width - 1 : width, :] * d_pre
    for k in range(width - 1):
        total = total + weight[k : k + 1, :] * shifted_up(d_pre, width - 1 - k)
    return total


def write_conv_grads(out_ref, d_pre, taps):
    for k, tap in enumerate(taps):
        out_ref[0, k : k + 1, :] = jnp.sum(d_pre * tap, axis=0, keepdims=True)
    out_ref[0, len(taps) : len(taps) + 1, :] = jnp.sum(d_pre, axis=0, keepdims=True)


def backward_kernel(
    width, heads, heads_here, head_size, blocks,
    x_ref, bc_ref, step_ref, cw_ref, cb_ref, cwbc_ref, cbbc_ref, head_ref, spread_ref, gather_ref,
    skip_ref, ssd_ref, dssd_ref,
    dx_ref, dbc_ref, dstep_ref, gx_ref, gbc_ref, ghead_ref,
    scores, d_scores, decay_cols, decay_rows, dt_scr, d_decay, d_dt, d_skip, act_bc,
):
    block = pl.program_id(1)
    span = x_ref.shape[0]
    state = bc_ref.shape[1] // 2
    half = span // 2

    @pl.when(block == 0)
    def _():
        pre = conv_pre_of(conv_taps(bc_ref[...], width), cwbc_ref[...], cbbc_ref[...])
        act = pre * jax.nn.sigmoid(pre)
        act_bc[...] = act.astype(bf16)
        scores[...] = dot32(act[:, :state], act[:, state:], ((1,), (1,)))
        prepare_steps(step_ref, head_ref, decay_cols, decay_rows, dt_scr, heads)
        d_scores[...] = jnp.zeros_like(d_scores)
        d_decay[...] = jnp.zeros_like(d_decay)
        d_dt[...] = jnp.zeros_like(d_dt)
        d_skip[...] = jnp.zeros_like(d_skip)

    taps = conv_taps(x_ref[...], width)
    pre = conv_pre_of(taps, cw_ref[...], cb_ref[...])
    sig = jax.nn.sigmoid(pre)
    xs = pre * sig
    dt_wide = dot32(dt_scr[...], spread_ref[...], ((1,), (0,)))
    weighted = (xs * dt_wide).astype(bf16)
    dy = dssd_ref[...]
    dy16 = dy.astype(bf16)
    lower = lax.broadcasted_iota(jnp.int32, (half, half), 0) <= lax.broadcasted_iota(
        jnp.int32, (half, half), 1
    )
    per_lane = LANES // head_size
    lane = lax.broadcasted_iota(jnp.int32, (span, LANES), 1)
    pieces = []
    for group in range(heads_here // per_lane):
        cols = slice(group * LANES, (group + 1) * LANES)
        wide = weighted[:, cols]
        dwide = dy16[:, cols]
        top_n, bottom_n, top_v, bottom_v = [], [], [], []
        for k in range(per_lane):
            h = block * heads_here + group * per_lane + k
            col = decay_cols[h]
            row = decay_rows[pl.ds(h, 1), :]
            p00 = jnp.exp(jnp.where(lower, row[:, :half] - col[:half, :half], MASKED))
            p01 = jnp.exp(row[:, half:] - col[:half, :half])
            p11 = jnp.exp(jnp.where(lower, row[:, half:] - col[half:, :half], MASKED))
            here = lane // head_size == k
            masked = jnp.where(here, wide, jnp.zeros_like(wide))
            dmasked = jnp.where(here, dwide, jnp.zeros_like(dwide))
            top = dot16(masked[:half], dwide, ((1,), (1,)))
            bottom = dot16(masked[half:], dwide[half:], ((1,), (1,)))
            d_scores[:half, :half] += top[:, :half] * p00
            d_scores[:half, half:] += top[:, half:] * p01
            d_scores[half:, half:] += bottom * p11
            top_n += [(scores[:half, :half] * p00).astype(bf16), (scores[:half, half:] * p01).astype(bf16)]
            top_v.append(dmasked)
            bottom_n.append((scores[half:, half:] * p11).astype(bf16))
            bottom_v.append(dmasked[half:])
        top = dot16(jnp.concatenate(top_n, 1), jnp.concatenate(top_v, 0), ((1,), (0,)))
        bottom = dot16(jnp.concatenate(bottom_n, 1), jnp.concatenate(bottom_v, 0), ((1,), (0,)))
        pieces.append(jnp.concatenate([top, bottom], 0))
    d_weighted = jnp.concatenate(pieces, 1)
    skip = skip_ref[...]
    inside = ssd_ref[...] - skip * xs
    crossing = dy16.astype(f32) * inside - weighted.astype(f32) * d_weighted
    high = crossing.astype(bf16)
    low = (crossing - high.astype(f32)).astype(bf16)
    d_decay[...] += dot16(high, gather_ref[...], ((1,), (0,))) + dot16(
        low, gather_ref[...], ((1,), (0,))
    )
    d_dt[...] += dot16((xs * d_weighted).astype(bf16), gather_ref[...], ((1,), (0,)))
    by_column = jnp.broadcast_to(jnp.sum(dy * xs, axis=0, keepdims=True), (8, dy.shape[1]))
    high = by_column.astype(bf16)
    low = (by_column - high.astype(f32)).astype(bf16)
    d_skip[...] += dot16(high, gather_ref[...], ((1,), (0,))) + dot16(
        low, gather_ref[...], ((1,), (0,))
    )
    d_xs = dt_wide * d_weighted + skip * dy
    d_pre = d_xs * (sig + xs * (1.0 - sig))
    write_conv_grads(gx_ref, d_pre, taps)
    dx_ref[...] = conv_back(d_pre, cw_ref[...], width).astype(bf16)

    @pl.when(block == blocks - 1)
    def _():
        rate = head_ref[1:2, :]
        dt = dt_scr[...]
        suffix = running_sum_back(d_decay[...])
        d_step = (d_dt[...] + rate * suffix) * jax.nn.sigmoid(step_ref[...] + head_ref[0:1, :])
        dstep_ref[...] = d_step.astype(bf16)
        ghead_ref[0, 0:1, :] = rate * jnp.sum(dt * suffix, axis=0, keepdims=True)
        ghead_ref[0, 1:2, :] = d_skip[0:1, :]
        ghead_ref[0, 2:3, :] = jnp.sum(d_step, axis=0, keepdims=True)
        d16 = d_scores[...].astype(bf16)
        d_b = dot16(d16, act_bc[:, state:], ((1,), (0,)))
        d_c = dot16(d16, act_bc[:, :state], ((0,), (0,)))
        taps = conv_taps(bc_ref[...], width)
        pre = conv_pre_of(taps, cwbc_ref[...], cbbc_ref[...])
        sig = jax.nn.sigmoid(pre)
        d_pre = jnp.concatenate([d_b, d_c], 1) * (sig + pre * sig * (1.0 - sig))
        write_conv_grads(gbc_ref, d_pre, taps)
        dbc_ref[...] = conv_back(d_pre, cwbc_ref[...], width).astype(bf16)


def mixer_specs(span, inner, state2, width_here):
    x_spec = pl.BlockSpec((span, width_here), lambda s, b: (s, b))
    bc_spec = pl.BlockSpec((span, state2), lambda s, b: (s, inner // state2))
    step_spec = pl.BlockSpec((span, LANES), lambda s, b: (s, 0))
    cw_spec = pl.BlockSpec((8, width_here), lambda s, b: (0, b))
    cb_spec = pl.BlockSpec((1, width_here), lambda s, b: (0, b))
    cwbc_spec = pl.BlockSpec((8, state2), lambda s, b: (0, inner // state2))
    cbbc_spec = pl.BlockSpec((1, state2), lambda s, b: (0, inner // state2))
    head_spec = pl.BlockSpec((8, LANES), lambda s, b: (0, 0))
    spread_spec = pl.BlockSpec((LANES, width_here), lambda s, b: (0, b))
    gather_spec = pl.BlockSpec((width_here, LANES), lambda s, b: (b, 0))
    return (x_spec, bc_spec, step_spec, cw_spec, cb_spec, cwbc_spec, cbbc_spec, head_spec, spread_spec, gather_spec)


def mixer_forward(px, step, cw, cb, head, spread, skip, sizes):
    span, inner, state2, heads, head_size, width, width_here = sizes
    seqs = px.shape[0] // span
    x_s, bc_s, st_s, cw_s, cb_s, cwbc_s, cbbc_s, hd_s, sp_s, _ = mixer_specs(span, inner, state2, width_here)
    return pl.pallas_call(
        functools.partial(forward_kernel, width, heads, width_here // head_size, head_size),
        grid=(seqs, inner // width_here),
        in_specs=[x_s, bc_s, st_s, cw_s, cb_s, cwbc_s, cbbc_s, hd_s, sp_s, cb_s],
        out_specs=x_s,
        out_shape=jax.ShapeDtypeStruct((px.shape[0], inner), f32),
        scratch_shapes=[
            pltpu.VMEM((span, span), f32),
            pltpu.VMEM((heads, span, LANES), f32),
            pltpu.VMEM((LANES, span), f32),
            pltpu.VMEM((span, LANES), f32),
        ],
        name="mixer_forward",
    )(px, px, step, cw, cb, cw, cb, head, spread, skip)


def mixer_backward(px, step, cw, cb, head, spread, gather, skip, ssd, dssd, sizes):
    span, inner, state2, heads, head_size, width, width_here = sizes
    seqs = px.shape[0] // span
    blocks = inner // width_here
    x_s, bc_s, st_s, cw_s, cb_s, cwbc_s, cbbc_s, hd_s, sp_s, ga_s = mixer_specs(span, inner, state2, width_here)
    return pl.pallas_call(
        functools.partial(
            backward_kernel, width, heads, width_here // head_size, head_size, blocks
        ),
        grid=(seqs, blocks),
        in_specs=[x_s, bc_s, st_s, cw_s, cb_s, cwbc_s, cbbc_s, hd_s, sp_s, ga_s, cb_s, x_s, x_s],
        out_specs=[
            x_s,
            pl.BlockSpec((span, state2), lambda s, b: (s, 0)),
            pl.BlockSpec((span, LANES), lambda s, b: (s, 0)),
            pl.BlockSpec((1, 8, width_here), lambda s, b: (s, 0, b)),
            pl.BlockSpec((1, 8, state2), lambda s, b: (s, 0, 0)),
            pl.BlockSpec((1, 8, LANES), lambda s, b: (s, 0, 0)),
        ],
        out_shape=[
            jax.ShapeDtypeStruct((px.shape[0], inner), bf16),
            jax.ShapeDtypeStruct((px.shape[0], state2), bf16),
            jax.ShapeDtypeStruct((px.shape[0], LANES), bf16),
            jax.ShapeDtypeStruct((seqs, 8, inner), f32),
            jax.ShapeDtypeStruct((seqs, 8, state2), f32),
            jax.ShapeDtypeStruct((seqs, 8, LANES), f32),
        ],
        scratch_shapes=[
            pltpu.VMEM((span, span), f32),
            pltpu.VMEM((span, span), f32),
            pltpu.VMEM((heads, span, LANES), f32),
            pltpu.VMEM((LANES, span), f32),
            pltpu.VMEM((span, LANES), f32),
            pltpu.VMEM((span, LANES), f32),
            pltpu.VMEM((span, LANES), f32),
            pltpu.VMEM((8, LANES), f32),
            pltpu.VMEM((span, state2), bf16),
        ],
        name="mixer_backward",
    )(px, px, step, cw, cb, cw, cb, head, spread, gather, skip, ssd, dssd)


def matmul(a, b, dims, kind=f32):
    return lax.dot_general(a, b, (dims, ((), ())), preferred_element_type=f32).astype(kind)


def on_device(
    counts,
    tokens, norm_gain, main_projection_weight, step_size_weight, conv_weight, conv_bias,
    a_log, d_skip, dt_bias, norm2_gain, output_projection_weight, cotangent,
):
    ny, nx, nz = counts
    plane = ny * nx
    devices = plane * 2 * nz
    core = lax.axis_index("core")
    micro, seqs_here, span, model = tokens.shape
    rows = main_projection_weight.shape[0]
    inner = norm2_gain.shape[0] * devices
    heads = a_log.shape[0]
    head_size = inner // heads
    width = conv_weight.shape[0]
    channels = conv_bias.shape[0] * devices
    state2 = channels - inner
    mine = inner // 2
    heads_mine = heads // 2
    own_tokens = micro * seqs_here * span

    def part_of(array, dim, which):
        size = array.shape[dim] // (plane * 2)
        split = array.reshape(array.shape[:dim] + (plane, 2, size) + array.shape[dim + 1 :])
        taken = lax.dynamic_index_in_dim(split, which, dim + 1, keepdims=False)
        return taken.reshape(array.shape[:dim] + (plane * size,) + array.shape[dim + 1 :])

    def whole_of(own, other, dim):
        size = own.shape[dim] // plane
        shape = own.shape[:dim] + (plane, size) + own.shape[dim + 1 :]
        own, other = own.reshape(shape), other.reshape(shape)
        first = core == 0
        both = jnp.stack([jnp.where(first, own, other), jnp.where(first, other, own)], axis=dim + 1)
        return both.reshape(both.shape[:dim] + (plane * 2 * size,) + both.shape[dim + 3 :])

    def embed(own, dim):
        return whole_of(own, jnp.zeros_like(own), dim)

    x_own = tokens.reshape(own_tokens, model)
    g_own = cotangent.reshape(own_tokens, model)

    small = jnp.concatenate(
        [
            norm_gain.reshape(-1), step_size_weight.reshape(-1), conv_weight.reshape(-1),
            conv_bias.reshape(-1), norm2_gain.reshape(-1),
        ]
    )
    used = small.shape[0]
    padded = -(-used // 2048) * 2048
    small = jnp.pad(small, (0, padded - used)).reshape(padded // LANES, LANES)
    small = line_gather(small, "core", 2, 0)
    small = line_gather(small, "z", nz, 1)
    small = line_gather(small, "x", nx, 0)
    small = line_gather(small, "y", ny, 0)
    small = small.reshape(devices, padded)
    at = 0
    taken = []
    for count in (rows, rows * heads, width * conv_bias.shape[0], conv_bias.shape[0], norm2_gain.shape[0]):
        taken.append(small[:, at : at + count])
        at += count
    gain = taken[0].reshape(1, model).astype(f32)
    step_weight = taken[1].reshape(model, heads)
    conv_w = jnp.swapaxes(taken[2].reshape(devices, width, -1), 0, 1).reshape(width, channels)
    conv_b = taken[3].reshape(1, channels)
    gain2 = part_of(taken[4].reshape(1, inner), 1, core).astype(f32)

    weight_z = main_projection_weight[:, :inner]
    weight_x = main_projection_weight[:, inner : 2 * inner]
    weight_bc = main_projection_weight[:, 2 * inner :]

    def columns_for(which):
        return (
            jnp.concatenate([part_of(weight_x, 1, which), weight_bc], axis=1),
            part_of(weight_z, 1, which),
        )

    keep_x, keep_z = columns_for(core)
    send_x, send_z = columns_for(1 - core)

    def pair_rows(keep, send):
        other = swap_core(send)
        first = core == 0
        return jnp.stack([jnp.where(first, keep, other), jnp.where(first, other, keep)])

    main_x = gather_chunk(pair_rows(keep_x, send_x), counts).reshape(model, mine + state2)
    main_z = gather_chunk(pair_rows(keep_z, send_z), counts).reshape(model, mine)
    out_weight = gather_chunk(output_projection_weight, counts).reshape(mine, model)

    x_all = jnp.concatenate([x_own, swap_core(x_own)], axis=0)
    g_all = jnp.concatenate([g_own, swap_core(g_own)], axis=0)

    inputs = x_all.astype(f32)
    inv_rms = lax.rsqrt(jnp.mean(inputs * inputs, axis=-1, keepdims=True) + epsilon)
    normed = (inputs * inv_rms * gain).astype(bf16)

    step_mine = jnp.pad(part_of(step_weight, 1, core), ((0, 0), (0, LANES - heads_mine)))
    px = matmul(normed, main_x, ((1,), (0,)))
    step = matmul(normed, step_mine, ((1,), (0,)))

    cw = jnp.concatenate([part_of(conv_w[:, :inner], 1, core), conv_w[:, inner:]], axis=1)
    cb = jnp.concatenate([part_of(conv_b[:, :inner], 1, core), conv_b[:, inner:]], axis=1).astype(f32)
    cw = jnp.pad(cw.astype(f32), ((0, 8 - width), (0, 0)))
    a_mine = part_of(a_log, 0, core)
    skip_mine = part_of(d_skip, 0, core)
    bias_mine = part_of(dt_bias, 0, core)
    head = jnp.pad(
        jnp.stack([bias_mine, -jnp.exp(a_mine)]), ((0, 6), (0, LANES - heads_mine))
    )
    spread = (
        lax.broadcasted_iota(jnp.int32, (LANES, mine), 0)
        == lax.broadcasted_iota(jnp.int32, (LANES, mine), 1) // head_size
    ).astype(f32)
    gather = spread.T.astype(bf16)
    skip = jnp.repeat(skip_mine, head_size).reshape(1, mine)
    width_here = 512 if mine % 512 == 0 else LANES
    sizes = (span, mine, state2, heads_mine, head_size, width, width_here)
    ssd = mixer_forward(px, step, cw, cb, head, spread, skip, sizes)

    def over_cores(partial):
        other = swap_core(partial)
        return partial + jnp.concatenate([other[own_tokens:], other[:own_tokens]], axis=0)

    z = matmul(normed, main_z, ((1,), (0,)))
    sig = jax.nn.sigmoid(z)
    v = ssd * z * sig
    q = lax.rsqrt(over_cores(jnp.sum(v * v, axis=-1, keepdims=True)) / inner + epsilon)
    gated = (v * q * gain2).astype(bf16)
    out_grad = matmul(gated, g_all, ((0,), (0,)), bf16)
    d_gated = matmul(g_all, out_weight, ((1,), (1,)))
    gain2_grad = jnp.sum(v * q * d_gated, axis=0)
    e = gain2 * d_gated
    shared = over_cores(jnp.sum(v * e, axis=-1, keepdims=True)) / inner
    d_v = q * e - v * (q * q * q) * shared
    d_ssd = d_v * z * sig
    d_z = (d_v * ssd * (sig + z * sig * (1.0 - sig))).astype(bf16)
    z_grad = matmul(normed, d_z, ((0,), (0,)), bf16)

    d_x, d_bc, d_step, conv_x, conv_bc, head_grads = mixer_backward(
        px, step, cw, cb, head, spread, gather, skip, ssd, d_ssd, sizes
    )
    d_conv = jnp.concatenate([d_x, d_bc], axis=1)
    x_grad = matmul(normed, d_conv, ((0,), (0,)), bf16)
    step_grad = matmul(normed, d_step, ((0,), (0,)))[:, :heads_mine]

    partial_out = matmul(gated, out_weight, ((1,), (0,)))
    out_total = partial_out[:own_tokens] + swap_core(partial_out[own_tokens:])
    block_out = (inputs[:own_tokens] + out_total).astype(bf16).reshape(tokens.shape)

    d_normed = (
        matmul(d_z, main_z, ((1,), (1,)))
        + matmul(d_conv, main_x, ((1,), (1,)))
        + matmul(d_step, step_mine, ((1,), (1,)))
    )
    d_normed = d_normed[:own_tokens] + swap_core(d_normed[own_tokens:])
    x_here, inv_here = inputs[:own_tokens], inv_rms[:own_tokens]
    gain_grad = jnp.sum(d_normed * x_here * inv_here, axis=0)
    scaled = d_normed * gain
    tokens_grad = (
        g_own.astype(f32)
        + inv_here * scaled
        - x_here * (inv_here * inv_here * inv_here) * jnp.mean(scaled * x_here, axis=-1, keepdims=True)
    ).reshape(tokens.shape)

    out_share = scatter_chunk(out_grad.reshape(ny, nx, nz, -1, model), counts).astype(f32)
    z_share = scatter_chunk(z_grad.reshape(ny, nx, 2, nz, rows, mine), counts)
    x_share = scatter_chunk(x_grad.reshape(ny, nx, 2, nz, rows, mine + state2), counts)

    def own_and_other(share):
        keep = lax.dynamic_index_in_dim(share, core, 0, keepdims=False)
        return keep, swap_core(lax.dynamic_index_in_dim(share, 1 - core, 0, keepdims=False))

    z_keep, z_other = own_and_other(z_share)
    x_keep, x_other = own_and_other(x_share)
    main_grad = jnp.concatenate(
        [
            whole_of(z_keep, z_other, 1).astype(f32),
            whole_of(x_keep[:, :mine], x_other[:, :mine], 1).astype(f32),
            x_keep[:, mine:].astype(f32) + x_other[:, mine:].astype(f32),
        ],
        axis=1,
    )

    conv_x = jnp.sum(conv_x, axis=0)
    conv_bc = jnp.sum(conv_bc, axis=0)
    conv_all = jnp.concatenate([embed(conv_x, 1), conv_bc], axis=1)
    conv_w_grad = jnp.swapaxes(conv_all[:width].reshape(width, devices, -1), 0, 1)
    packed = jnp.concatenate(
        [
            gain_grad.reshape(devices, -1),
            embed(step_grad, 1).reshape(devices, -1),
            conv_w_grad.reshape(devices, -1),
            conv_all[width].reshape(devices, -1),
            embed(gain2_grad, 0).reshape(devices, -1),
        ],
        axis=1,
    )
    packed = jnp.pad(packed, ((0, 0), (0, padded - used)))
    packed = packed.reshape(ny, nx, 2, nz, padded // LANES, LANES)
    packed = line_scatter(packed, "core", 2, 2)
    packed = line_scatter(packed, "x", nx, 1)
    packed = line_scatter(packed, "y", ny, 0)
    packed = line_scatter(packed, "z", nz, 0).reshape(-1)
    at = 0
    small_grads = []
    for shape in (
        norm_gain.shape, step_size_weight.shape, conv_weight.shape, conv_bias.shape, norm2_gain.shape,
    ):
        count = 1
        for dim in shape:
            count *= dim
        small_grads.append(packed[at : at + count].reshape(shape))
        at += count

    head_sums = embed(jnp.sum(head_grads, axis=0)[:3, :heads_mine], 1)
    head_sums = jnp.pad(head_sums, ((0, 5), (0, LANES - heads)))
    for axis, count in (("core", 2), ("x", nx), ("y", ny), ("z", nz)):
        head_sums = jnp.sum(line_gather(head_sums, axis, count, 0), axis=0)

    return (
        block_out,
        tokens_grad,
        small_grads[0],
        main_grad,
        small_grads[1],
        small_grads[2],
        small_grads[3],
        head_sums[0, :heads],
        head_sums[1, :heads],
        head_sums[2, :heads],
        small_grads[4],
        out_share,
    )


def solution(mesh):
    dp, fsdp = mesh.shape["dp"], mesh.shape["fsdp"]
    counts = (2, dp // 4, fsdp)
    split = Mesh(mesh.devices.reshape(2, dp // 4, 2, fsdp), ALL_AXES)
    in_specs = (
        P(None, ALL_AXES, None, None),
        P(ALL_AXES),
        P(ALL_AXES, None),
        P(ALL_AXES, None),
        P(None, ALL_AXES),
        P(ALL_AXES),
        P(),
        P(),
        P(),
        P(ALL_AXES),
        P(ALL_AXES, None),
        P(None, ALL_AXES, None, None),
    )
    out_specs = (
        P(None, ALL_AXES, None, None),
        P(None, ALL_AXES, None, None),
        P(ALL_AXES),
        P(ALL_AXES, None),
        P(ALL_AXES, None),
        P(None, ALL_AXES),
        P(ALL_AXES),
        P(),
        P(),
        P(),
        P(ALL_AXES),
        P(ALL_AXES, None),
    )
    return jax.shard_map(
        functools.partial(on_device, counts),
        mesh=split, in_specs=in_specs, out_specs=out_specs, check_vma=False,
    )
```

```python
import functools

import jax
import jax.numpy as jnp
from jax import lax
from jax.experimental import pallas as pl
from jax.experimental.pallas import tpu as pltpu
from jax.sharding import Mesh
from jax.sharding import PartitionSpec as P


epsilon = 1e-05
f32 = jnp.float32
bf16 = jnp.bfloat16
LANES = 128
ALL_AXES = ("y", "x", "core", "z")


def swap_core(array):
    return lax.ppermute(array, "core", [(0, 1), (1, 0)])


def bits_of(axis, count):
    digits = []
    bit = count // 2
    while bit >= 1:
        digits.append((ALL_AXES.index(axis), -bit, axis, bit, count))
        bit //= 2
    return digits


def exchange(array, digit):
    _, _, axis, bit, count = digit
    return lax.ppermute(array, axis, [(i, i ^ bit) for i in range(count)])


def digit_here(digit):
    _, _, axis, bit, _ = digit
    return lax.rem(lax.axis_index(axis) // bit, 2)


def gather_stage(array, held, digit):
    other = exchange(array, digit)
    place = sum(1 for d in held if d < digit)
    first = digit_here(digit) == 0
    joined = jnp.stack([jnp.where(first, array, other), jnp.where(first, other, array)], axis=place)
    return joined, sorted(held + [digit])


def scatter_send(array, held, digit):
    place = held.index(digit)
    send = lax.dynamic_index_in_dim(array, 1 - digit_here(digit), place, keepdims=False)
    return exchange(send, digit)


def scatter_add(array, held, digit, other):
    place = held.index(digit)
    keep = lax.dynamic_index_in_dim(array, digit_here(digit), place, keepdims=False)
    total = (keep.astype(f32) + other.astype(f32)).astype(array.dtype)
    return total, [d for d in held if d != digit]


def column_parts(array):
    cut = array.shape[-1] // 2 // LANES * LANES
    return array[..., :cut], array[..., cut:]


def routes(counts):
    ny, nx, nz = counts
    y, x = bits_of("y", ny), bits_of("x", nx)
    return bits_of("z", nz), (y + x, x + y)


def gather_start(shard, held, counts):
    for digit in routes(counts)[0]:
        shard, held = gather_stage(shard, held, digit)
    return shard, held


def gather_finish(shard, held, counts):
    orders = routes(counts)[1]
    parts = list(column_parts(shard))
    keep = [held, held]
    for i in range(len(orders[0])):
        for p in range(2):
            parts[p], keep[p] = gather_stage(parts[p], keep[p], orders[p][i])
    return jnp.concatenate(parts, axis=-1)


def scatter_chunk(grads, held, counts):
    digits, orders = routes(counts)
    parts = list(column_parts(grads))
    keep = [held, held]
    for i in range(len(orders[0])):
        got = [scatter_send(parts[p], keep[p], orders[1 - p][i]) for p in range(2)]
        for p in range(2):
            parts[p], keep[p] = scatter_add(parts[p], keep[p], orders[1 - p][i], got[p])
    both, held = jnp.concatenate(parts, axis=-1), keep[0]
    for digit in reversed(digits):
        got = scatter_send(both, held, digit)
        both, held = scatter_add(both, held, digit, got)
    return both


def spread_blocks(array, axes, count):
    return lax.all_to_all(jnp.broadcast_to(array, (count,) + array.shape), axes, 0, 0)


def sum_blocks(array, axes):
    got = lax.all_to_all(array, axes, 0, 0)
    return jnp.sum(got.astype(f32), axis=0).astype(array.dtype)


def shifted_down(values, steps):
    rows = lax.broadcasted_iota(jnp.int32, values.shape, 0)
    return jnp.where(rows >= steps, pltpu.roll(values, steps, 0), 0.0)


def shifted_up(values, steps):
    count = values.shape[0]
    rows = lax.broadcasted_iota(jnp.int32, values.shape, 0)
    return jnp.where(rows < count - steps, pltpu.roll(values, count - steps, 0), 0.0)


def running_sum(values):
    step = 1
    while step < values.shape[0]:
        values = values + shifted_down(values, step)
        step *= 2
    return values


def running_sum_back(values):
    step = 1
    while step < values.shape[0]:
        values = values + shifted_up(values, step)
        step *= 2
    return values


def conv_taps(values, width):
    return [values if k == width - 1 else shifted_down(values, width - 1 - k) for k in range(width)]


def conv_pre_of(taps, weight, bias):
    total = bias + weight[0:1, :] * taps[0]
    for k in range(1, len(taps)):
        total = total + weight[k : k + 1, :] * taps[k]
    return total


def dot32(a, b, dims):
    return lax.dot_general(
        a, b, (dims, ((), ())), precision=lax.Precision.HIGHEST, preferred_element_type=f32
    )


def dot16(a, b, dims):
    return lax.dot_general(a, b, (dims, ((), ())), preferred_element_type=f32)


def softplus(v):
    return jnp.maximum(v, 0.0) + jnp.log1p(jnp.exp(-jnp.abs(v)))


MASKED = -1e30


def prepare_steps(step_ref, head_ref, decay_cols, decay_rows, dt_scr, first, last):
    dt = softplus(step_ref[...] + head_ref[0:1, :])
    dt_scr[...] = dt
    decay = running_sum(dt * head_ref[1:2, :])
    decay_rows[...] = decay.T
    for h in range(first, last):
        decay_cols[h - first] = jnp.broadcast_to(decay[:, h : h + 1], (decay.shape[0], LANES))


def forward_kernel(
    width, heads, heads_here, head_size,
    x_ref, bc_ref, step_ref, cw_ref, cb_ref, cwbc_ref, cbbc_ref, head_ref, spread_ref, skip_ref,
    out_ref, scores, decay_cols, decay_rows, dt_scr,
):
    block = pl.program_id(1)
    span = x_ref.shape[0]
    state = bc_ref.shape[1] // 2
    half = span // 2

    @pl.when(block == 0)
    def _():
        pre = conv_pre_of(conv_taps(bc_ref[...], width), cwbc_ref[...], cbbc_ref[...])
        act = pre * jax.nn.sigmoid(pre)
        scores[...] = dot32(act[:, state:], act[:, :state], ((1,), (1,)))
        prepare_steps(step_ref, head_ref, decay_cols, decay_rows, dt_scr, 0, heads)

    pre = conv_pre_of(conv_taps(x_ref[...], width), cw_ref[...], cb_ref[...])
    xs = pre * jax.nn.sigmoid(pre)
    weighted = (xs * dot32(dt_scr[...], spread_ref[...], ((1,), (0,)))).astype(bf16)
    lower = lax.broadcasted_iota(jnp.int32, (half, half), 0) >= lax.broadcasted_iota(
        jnp.int32, (half, half), 1
    )
    per_lane = LANES // head_size
    lane = lax.broadcasted_iota(jnp.int32, (span, LANES), 1)
    for group in range(heads_here // per_lane):
        cols = slice(group * LANES, (group + 1) * LANES)
        wide = weighted[:, cols]
        top_n, bottom_n, top_v, bottom_v = [], [], [], []
        for k in range(per_lane):
            h = block * heads_here + group * per_lane + k
            col = decay_cols[h]
            row = decay_rows[pl.ds(h, 1), :]
            gap = jnp.where(lower, col[:half, :half] - row[:, :half], MASKED)
            n00 = (scores[:half, :half] * jnp.exp(gap)).astype(bf16)
            n10 = (scores[half:, :half] * jnp.exp(col[half:, :half] - row[:, :half])).astype(bf16)
            gap = jnp.where(lower, col[half:, :half] - row[:, half:], MASKED)
            n11 = (scores[half:, half:] * jnp.exp(gap)).astype(bf16)
            masked = jnp.where(lane // head_size == k, wide, jnp.zeros_like(wide))
            top_n.append(n00)
            top_v.append(masked[:half])
            bottom_n += [n10, n11]
            bottom_v.append(masked)
        top = dot16(jnp.concatenate(top_n, 1), jnp.concatenate(top_v, 0), ((1,), (0,)))
        bottom = dot16(jnp.concatenate(bottom_n, 1), jnp.concatenate(bottom_v, 0), ((1,), (0,)))
        skip = skip_ref[:, cols]
        out_ref[:half, cols] = top + skip * xs[:half, cols]
        out_ref[half:, cols] = bottom + skip * xs[half:, cols]


def conv_back(d_pre, weight, width):
    total = weight[width - 1 : width, :] * d_pre
    for k in range(width - 1):
        total = total + weight[k : k + 1, :] * shifted_up(d_pre, width - 1 - k)
    return total


def write_conv_grads(out_ref, d_pre, taps):
    for k, tap in enumerate(taps):
        out_ref[0, k : k + 1, :] = jnp.sum(d_pre * tap, axis=0, keepdims=True)
    out_ref[0, len(taps) : len(taps) + 1, :] = jnp.sum(d_pre, axis=0, keepdims=True)


def backward_kernel(
    width, heads_here, head_size, blocks, first_block, last_call,
    x_ref, bc_ref, step_ref, cw_ref, cb_ref, cwbc_ref, cbbc_ref, head_ref, spread_ref, gather_ref,
    skip_ref, ssd_ref, dssd_ref, *refs,
):
    if last_call:
        d_scores_in, d_decay_in, d_dt_in, d_skip_in = refs[:4]
        dp_ref, gx_ref, gbc_ref, ghead_ref = refs[4:8]
        d_scores, d_decay, d_dt, d_skip = refs[8:12]
    else:
        dp_ref, gx_ref, d_scores, d_decay, d_dt, d_skip = refs[:6]
    scores, decay_cols, decay_rows, dt_scr, act_bc = refs[-5:]
    block = pl.program_id(1)
    span = x_ref.shape[0]
    state = bc_ref.shape[1] // 2
    half = span // 2
    first_head = first_block * heads_here

    @pl.when(block == 0)
    def _():
        pre = conv_pre_of(conv_taps(bc_ref[...], width), cwbc_ref[...], cbbc_ref[...])
        act = pre * jax.nn.sigmoid(pre)
        act_bc[...] = act.astype(bf16)
        scores[...] = dot32(act[:, :state], act[:, state:], ((1,), (1,)))
        prepare_steps(
            step_ref, head_ref, decay_cols, decay_rows, dt_scr,
            first_head, first_head + blocks * heads_here,
        )
        if last_call:
            d_scores[...] = d_scores_in[...]
            d_decay[...] = d_decay_in[...]
            d_dt[...] = d_dt_in[...]
            d_skip[...] = d_skip_in[...]
        else:
            d_scores[...] = jnp.zeros_like(d_scores)
            d_decay[...] = jnp.zeros_like(d_decay)
            d_dt[...] = jnp.zeros_like(d_dt)
            d_skip[...] = jnp.zeros_like(d_skip)

    taps = conv_taps(x_ref[...], width)
    pre = conv_pre_of(taps, cw_ref[...], cb_ref[...])
    sig = jax.nn.sigmoid(pre)
    xs = pre * sig
    dt_wide = dot32(dt_scr[...], spread_ref[...], ((1,), (0,)))
    weighted = (xs * dt_wide).astype(bf16)
    dy = dssd_ref[...]
    dy16 = dy.astype(bf16)
    lower = lax.broadcasted_iota(jnp.int32, (half, half), 0) <= lax.broadcasted_iota(
        jnp.int32, (half, half), 1
    )
    per_lane = LANES // head_size
    lane = lax.broadcasted_iota(jnp.int32, (span, LANES), 1)
    pieces = []
    for group in range(heads_here // per_lane):
        cols = slice(group * LANES, (group + 1) * LANES)
        wide = weighted[:, cols]
        dwide = dy16[:, cols]
        top_n, bottom_n, top_v, bottom_v = [], [], [], []
        for k in range(per_lane):
            h = block * heads_here + group * per_lane + k
            col = decay_cols[h]
            row = decay_rows[pl.ds(first_head + h, 1), :]
            p00 = jnp.exp(jnp.where(lower, row[:, :half] - col[:half, :half], MASKED))
            p01 = jnp.exp(row[:, half:] - col[:half, :half])
            p11 = jnp.exp(jnp.where(lower, row[:, half:] - col[half:, :half], MASKED))
            here = lane // head_size == k
            masked = jnp.where(here, wide, jnp.zeros_like(wide))
            dmasked = jnp.where(here, dwide, jnp.zeros_like(dwide))
            top = dot16(masked[:half], dwide, ((1,), (1,)))
            bottom = dot16(masked[half:], dwide[half:], ((1,), (1,)))
            d_scores[:half, :half] += top[:, :half] * p00
            d_scores[:half, half:] += top[:, half:] * p01
            d_scores[half:, half:] += bottom * p11
            top_n += [(scores[:half, :half] * p00).astype(bf16), (scores[:half, half:] * p01).astype(bf16)]
            top_v.append(dmasked)
            bottom_n.append((scores[half:, half:] * p11).astype(bf16))
            bottom_v.append(dmasked[half:])
        top = dot16(jnp.concatenate(top_n, 1), jnp.concatenate(top_v, 0), ((1,), (0,)))
        bottom = dot16(jnp.concatenate(bottom_n, 1), jnp.concatenate(bottom_v, 0), ((1,), (0,)))
        pieces.append(jnp.concatenate([top, bottom], 0))
    d_weighted = jnp.concatenate(pieces, 1)
    skip = skip_ref[...]
    inside = ssd_ref[...] - skip * xs
    crossing = dy16.astype(f32) * inside - weighted.astype(f32) * d_weighted
    high = crossing.astype(bf16)
    low = (crossing - high.astype(f32)).astype(bf16)
    d_decay[...] += dot16(high, gather_ref[...], ((1,), (0,))) + dot16(
        low, gather_ref[...], ((1,), (0,))
    )
    d_dt[...] += dot16((xs * d_weighted).astype(bf16), gather_ref[...], ((1,), (0,)))
    by_column = jnp.broadcast_to(jnp.sum(dy * xs, axis=0, keepdims=True), (8, dy.shape[1]))
    high = by_column.astype(bf16)
    low = (by_column - high.astype(f32)).astype(bf16)
    d_skip[...] += dot16(high, gather_ref[...], ((1,), (0,))) + dot16(
        low, gather_ref[...], ((1,), (0,))
    )
    d_xs = dt_wide * d_weighted + skip * dy
    d_pre = d_xs * (sig + xs * (1.0 - sig))
    write_conv_grads(gx_ref, d_pre, taps)
    wide = x_ref.shape[1]
    dp_ref[:, pl.ds(pl.multiple_of(block * wide, wide), wide)] = conv_back(
        d_pre, cw_ref[...], width
    ).astype(bf16)

    if not last_call:
        return

    @pl.when(block == blocks - 1)
    def _():
        rate = head_ref[1:2, :]
        dt = dt_scr[...]
        suffix = running_sum_back(d_decay[...])
        d_step = (d_dt[...] + rate * suffix) * jax.nn.sigmoid(step_ref[...] + head_ref[0:1, :])
        inner = wide * blocks
        dp_ref[:, inner + 2 * state :] = d_step.astype(bf16)
        ghead_ref[0, 0:1, :] = rate * jnp.sum(dt * suffix, axis=0, keepdims=True)
        ghead_ref[0, 1:2, :] = d_skip[0:1, :]
        ghead_ref[0, 2:3, :] = jnp.sum(d_step, axis=0, keepdims=True)
        d16 = d_scores[...].astype(bf16)
        d_b = dot16(d16, act_bc[:, state:], ((1,), (0,)))
        d_c = dot16(d16, act_bc[:, :state], ((0,), (0,)))
        taps = conv_taps(bc_ref[...], width)
        pre = conv_pre_of(taps, cwbc_ref[...], cbbc_ref[...])
        sig = jax.nn.sigmoid(pre)
        d_pre = jnp.concatenate([d_b, d_c], 1) * (sig + pre * sig * (1.0 - sig))
        write_conv_grads(gbc_ref, d_pre, taps)
        dp_ref[:, inner : inner + 2 * state] = conv_back(d_pre, cwbc_ref[...], width).astype(bf16)


def mixer_specs(span, inner, state2, width_here, first):
    x_spec = pl.BlockSpec((span, width_here), lambda s, b: (s, first + b))
    bc_spec = pl.BlockSpec((span, state2), lambda s, b: (s, inner // state2))
    step_spec = pl.BlockSpec((span, LANES), lambda s, b: (s, (inner + state2) // LANES))
    cw_spec = pl.BlockSpec((8, width_here), lambda s, b: (0, first + b))
    cb_spec = pl.BlockSpec((1, width_here), lambda s, b: (0, first + b))
    cwbc_spec = pl.BlockSpec((8, state2), lambda s, b: (0, inner // state2))
    cbbc_spec = pl.BlockSpec((1, state2), lambda s, b: (0, inner // state2))
    head_spec = pl.BlockSpec((8, LANES), lambda s, b: (0, 0))
    spread_spec = pl.BlockSpec((LANES, width_here), lambda s, b: (0, first + b))
    gather_spec = pl.BlockSpec((width_here, LANES), lambda s, b: (first + b, 0))
    return (x_spec, bc_spec, step_spec, cw_spec, cb_spec, cwbc_spec, cbbc_spec, head_spec, spread_spec, gather_spec)


def mixer_forward(px, cw, cb, head, spread, skip, sizes):
    span, inner, state2, heads, head_size, width, width_here, _ = sizes
    seqs = px.shape[0] // span
    x_s, bc_s, st_s, cw_s, cb_s, cwbc_s, cbbc_s, hd_s, sp_s, _ = mixer_specs(span, inner, state2, width_here, 0)
    return pl.pallas_call(
        functools.partial(forward_kernel, width, heads, width_here // head_size, head_size),
        grid=(seqs, inner // width_here),
        in_specs=[x_s, bc_s, st_s, cw_s, cb_s, cwbc_s, cbbc_s, hd_s, sp_s, cb_s],
        out_specs=x_s,
        out_shape=jax.ShapeDtypeStruct((px.shape[0], inner), f32),
        scratch_shapes=[
            pltpu.VMEM((span, span), f32),
            pltpu.VMEM((heads, span, LANES), f32),
            pltpu.VMEM((LANES, span), f32),
            pltpu.VMEM((span, LANES), f32),
        ],
        name="mixer_forward",
    )(px, px, px, cw, cb, cw, cb, head, spread, skip)


def mixer_backward(px, cw, cb, head, spread, gather, skip, ssd, dssd, sizes, carried):
    span, inner, state2, heads, head_size, width, _, width_here = sizes
    seqs = px.shape[0] // span
    blocks = inner // width_here // 2
    last_call = carried is not None
    first = blocks if last_call else 0
    x_s, bc_s, st_s, cw_s, cb_s, cwbc_s, cbbc_s, hd_s, sp_s, ga_s = mixer_specs(
        span, inner, state2, width_here, first
    )
    columns = inner // 2 + (state2 + LANES if last_call else 0)
    sum_shapes = [(span, span), (span, LANES), (span, LANES), (8, LANES)]
    sum_specs = [pl.BlockSpec(shape, lambda s, b: (s, 0)) for shape in sum_shapes]
    in_specs = [x_s, bc_s, st_s, cw_s, cb_s, cwbc_s, cbbc_s, hd_s, sp_s, ga_s, cb_s, x_s, x_s]
    out_specs = [
        pl.BlockSpec((span, columns), lambda s, b: (s, 0)),
        pl.BlockSpec((1, 8, width_here), lambda s, b: (s, 0, b)),
    ]
    out_shape = [
        jax.ShapeDtypeStruct((px.shape[0], columns), bf16),
        jax.ShapeDtypeStruct((seqs, 8, inner // 2), f32),
    ]
    scratch = [
        pltpu.VMEM((span, span), f32),
        pltpu.VMEM((heads // 2, span, LANES), f32),
        pltpu.VMEM((LANES, span), f32),
        pltpu.VMEM((span, LANES), f32),
        pltpu.VMEM((span, state2), bf16),
    ]
    if last_call:
        in_specs += sum_specs
        out_specs += [
            pl.BlockSpec((1, 8, state2), lambda s, b: (s, 0, 0)),
            pl.BlockSpec((1, 8, LANES), lambda s, b: (s, 0, 0)),
        ]
        out_shape += [
            jax.ShapeDtypeStruct((seqs, 8, state2), f32),
            jax.ShapeDtypeStruct((seqs, 8, LANES), f32),
        ]
        scratch = [pltpu.VMEM(shape, f32) for shape in sum_shapes] + scratch
    else:
        out_specs += sum_specs
        out_shape += [jax.ShapeDtypeStruct((seqs * shape[0], shape[1]), f32) for shape in sum_shapes]
    return pl.pallas_call(
        functools.partial(
            backward_kernel, width, width_here // head_size, head_size, blocks, first, last_call
        ),
        grid=(seqs, blocks),
        in_specs=in_specs,
        out_specs=out_specs,
        out_shape=out_shape,
        scratch_shapes=scratch,
        name="mixer_backward_b" if last_call else "mixer_backward_a",
    )(px, px, px, cw, cb, cw, cb, head, spread, gather, skip, ssd, dssd, *(carried or ()))


def matmul(a, b, dims, kind=f32):
    return lax.dot_general(a, b, (dims, ((), ())), preferred_element_type=f32).astype(kind)


def on_device(
    counts,
    tokens, norm_gain, main_projection_weight, step_size_weight, conv_weight, conv_bias,
    a_log, d_skip, dt_bias, norm2_gain, output_projection_weight, cotangent,
):
    ny, nx, nz = counts
    plane = ny * nx
    devices = plane * 2 * nz
    core = lax.axis_index("core")
    micro, seqs_here, span, model = tokens.shape
    rows = main_projection_weight.shape[0]
    inner = norm2_gain.shape[0] * devices
    heads = a_log.shape[0]
    head_size = inner // heads
    width = conv_weight.shape[0]
    channels = conv_bias.shape[0] * devices
    state2 = channels - inner
    mine = inner // 2
    heads_mine = heads // 2
    own_tokens = micro * seqs_here * span

    def part_of(array, dim, which):
        size = array.shape[dim] // (plane * 2)
        split = array.reshape(array.shape[:dim] + (plane, 2, size) + array.shape[dim + 1 :])
        taken = lax.dynamic_index_in_dim(split, which, dim + 1, keepdims=False)
        return taken.reshape(array.shape[:dim] + (plane * size,) + array.shape[dim + 1 :])

    def whole_of(own, other, dim):
        size = own.shape[dim] // plane
        shape = own.shape[:dim] + (plane, size) + own.shape[dim + 1 :]
        own, other = own.reshape(shape), other.reshape(shape)
        first = core == 0
        both = jnp.stack([jnp.where(first, own, other), jnp.where(first, other, own)], axis=dim + 1)
        return both.reshape(both.shape[:dim] + (plane * 2 * size,) + both.shape[dim + 3 :])

    def embed(own, dim):
        return whole_of(own, jnp.zeros_like(own), dim)

    x_own = tokens.reshape(own_tokens, model)
    g_own = cotangent.reshape(own_tokens, model)

    weight_z = main_projection_weight[:, :inner]
    weight_x = main_projection_weight[:, inner : 2 * inner]
    weight_bc = main_projection_weight[:, 2 * inner :]

    def columns_for(which):
        steps = part_of(step_size_weight, 1, which)
        steps = jnp.pad(steps, ((0, 0), (0, LANES - heads_mine)))
        x_part = jnp.concatenate([part_of(weight_x, 1, which), weight_bc, steps], axis=1)
        return x_part, part_of(weight_z, 1, which)

    keep_x, keep_z = columns_for(core)
    send_x, send_z = columns_for(1 - core)

    core_digit = bits_of("core", 2)[0]

    def pair_rows(keep, send):
        other = swap_core(send)
        first = core == 0
        return jnp.stack([jnp.where(first, keep, other), jnp.where(first, other, keep)])

    pair_x = pair_rows(keep_x, send_x)
    part_x, held_x = gather_start(pair_x, [core_digit], counts)
    main_x = gather_finish(part_x, held_x, counts).reshape(model, mine + state2 + LANES)
    pair_z = pair_rows(keep_z, send_z)
    part_z, held_z = gather_start(pair_z, [core_digit], counts)
    main_z = gather_finish(part_z, held_z, counts).reshape(model, mine)
    part_o, held_o = gather_start(output_projection_weight, [], counts)
    out_weight = gather_finish(part_o, held_o, counts).reshape(mine, model)

    small = jnp.concatenate(
        [
            norm_gain.reshape(-1), conv_weight.reshape(-1), conv_bias.reshape(-1), norm2_gain.reshape(-1),
        ]
    )
    used = small.shape[0]
    padded = -(-used // 1024) * 1024
    small = jnp.pad(small, (0, padded - used)).reshape(padded // LANES, LANES)
    small = spread_blocks(small, ALL_AXES, devices).reshape(devices, padded)
    at = 0
    taken = []
    for count in (rows, width * conv_bias.shape[0], conv_bias.shape[0], norm2_gain.shape[0]):
        taken.append(small[:, at : at + count])
        at += count
    gain = taken[0].reshape(1, model).astype(f32)
    conv_w = jnp.swapaxes(taken[1].reshape(devices, width, -1), 0, 1).reshape(width, channels)
    conv_b = taken[2].reshape(1, channels)
    gain2 = part_of(taken[3].reshape(1, inner), 1, core).astype(f32)

    x_all = jnp.concatenate([x_own, swap_core(x_own)], axis=0)
    g_all = jnp.concatenate([g_own, swap_core(g_own)], axis=0)

    inputs = x_all.astype(f32)
    inv_rms = lax.rsqrt(jnp.mean(inputs * inputs, axis=-1, keepdims=True) + epsilon)
    normed = (inputs * inv_rms * gain).astype(bf16)
    px = matmul(normed, main_x, ((1,), (0,)))

    cw = jnp.concatenate([part_of(conv_w[:, :inner], 1, core), conv_w[:, inner:]], axis=1)
    cb = jnp.concatenate([part_of(conv_b[:, :inner], 1, core), conv_b[:, inner:]], axis=1).astype(f32)
    cw = jnp.pad(cw.astype(f32), ((0, 8 - width), (0, 0)))
    a_mine = part_of(a_log, 0, core)
    skip_mine = part_of(d_skip, 0, core)
    bias_mine = part_of(dt_bias, 0, core)
    head = jnp.pad(
        jnp.stack([bias_mine, -jnp.exp(a_mine)]), ((0, 6), (0, LANES - heads_mine))
    )
    spread = (
        lax.broadcasted_iota(jnp.int32, (LANES, mine), 0)
        == lax.broadcasted_iota(jnp.int32, (LANES, mine), 1) // head_size
    ).astype(f32)
    gather = spread.T.astype(bf16)
    skip = jnp.repeat(skip_mine, head_size).reshape(1, mine)
    sizes = (span, mine, state2, heads_mine, head_size, width, mine // 3, mine // 4)
    ssd = mixer_forward(px, cw, cb, head, spread, skip, sizes)

    def over_cores(partial):
        other = swap_core(partial)
        return partial + jnp.concatenate([other[own_tokens:], other[:own_tokens]], axis=0)

    z = matmul(normed, main_z, ((1,), (0,)))
    sig = jax.nn.sigmoid(z)
    v = ssd * z * sig
    squares = jnp.sum(v * v, axis=-1, keepdims=True)
    squares = over_cores(squares)
    q = lax.rsqrt(squares / inner + epsilon)
    gated = (v * q * gain2).astype(bf16)
    out_grad = matmul(gated, g_all, ((0,), (0,)), bf16)
    d_gated = matmul(g_all, out_weight, ((1,), (1,)))
    gain2_grad = jnp.sum(v * q * d_gated, axis=0)
    e = gain2 * d_gated
    shared = jnp.sum(v * e, axis=-1, keepdims=True)
    shared = over_cores(shared) / inner
    d_v = q * e - v * (q * q * q) * shared
    d_ssd = d_v * z * sig
    d_z = (d_v * ssd * (sig + z * sig * (1.0 - sig))).astype(bf16)
    z_grad = matmul(normed, d_z, ((0,), (0,)), bf16)

    d_pa, conv_a, *carried = mixer_backward(
        px, cw, cb, head, spread, gather, skip, ssd, d_ssd, sizes, None
    )
    a_grad = matmul(normed, d_pa, ((0,), (0,)), bf16)
    d_pb, conv_b2, conv_bc, head_grads = mixer_backward(
        px, cw, cb, head, spread, gather, skip, ssd, d_ssd, sizes, carried
    )
    b_grad = matmul(normed, d_pb, ((0,), (0,)), bf16)
    conv_x = jnp.concatenate([conv_a, conv_b2], axis=2)

    partial_out = matmul(gated, out_weight, ((1,), (0,)))
    out_total = partial_out[:own_tokens] + swap_core(partial_out[own_tokens:])
    block_out = (inputs[:own_tokens] + out_total).astype(bf16).reshape(tokens.shape)

    d_normed = (
        matmul(d_z, main_z, ((1,), (1,)))
        + matmul(d_pa, main_x[:, : mine // 2], ((1,), (1,)))
        + matmul(d_pb, main_x[:, mine // 2 :], ((1,), (1,)))
    )
    d_normed = d_normed[:own_tokens] + swap_core(d_normed[own_tokens:])
    x_here, inv_here = inputs[:own_tokens], inv_rms[:own_tokens]
    gain_grad = jnp.sum(d_normed * x_here * inv_here, axis=0)
    scaled = d_normed * gain
    tokens_grad = (
        g_own.astype(f32)
        + inv_here * scaled
        - x_here * (inv_here * inv_here * inv_here) * jnp.mean(scaled * x_here, axis=-1, keepdims=True)
    ).reshape(tokens.shape)

    digits, orders = routes(counts)
    plane_digits = orders[0]
    two = (2,) * (len(plane_digits))
    twoz = (2,) * (len(digits))
    out_share = scatter_chunk(
        out_grad.reshape(two + twoz + (-1, model)), plane_digits + digits, counts
    ).astype(f32)
    held = plane_digits + [core_digit] + digits
    z_share = scatter_chunk(z_grad.reshape(two + (2,) + twoz + (rows, -1)), held, counts)
    a_share = scatter_chunk(a_grad.reshape(two + (2,) + twoz + (rows, -1)), held, counts)
    b_share = scatter_chunk(b_grad.reshape(two + (2,) + twoz + (rows, -1)), held, counts)
    x_share = jnp.concatenate([a_share, b_share], axis=-1)

    def own_and_other(share):
        keep = lax.dynamic_index_in_dim(share, core, 0, keepdims=False)
        return keep, swap_core(lax.dynamic_index_in_dim(share, 1 - core, 0, keepdims=False))

    z_keep, z_other = own_and_other(z_share)
    x_keep, x_other = own_and_other(x_share)
    main_grad = jnp.concatenate(
        [
            whole_of(z_keep, z_other, 1).astype(f32),
            whole_of(x_keep[:, :mine], x_other[:, :mine], 1).astype(f32),
            x_keep[:, mine : mine + state2].astype(f32) + x_other[:, mine : mine + state2].astype(f32),
        ],
        axis=1,
    )
    steps = slice(mine + state2, mine + state2 + heads_mine)
    step_grad = whole_of(x_keep[:, steps], x_other[:, steps], 1).astype(f32)

    conv_x = jnp.sum(conv_x, axis=0)
    conv_bc = jnp.sum(conv_bc, axis=0)
    conv_all = jnp.concatenate([embed(conv_x, 1), conv_bc], axis=1)
    conv_w_grad = jnp.swapaxes(conv_all[:width].reshape(width, devices, -1), 0, 1)
    packed = jnp.concatenate(
        [
            gain_grad.reshape(devices, -1),
            conv_w_grad.reshape(devices, -1),
            conv_all[width].reshape(devices, -1),
            embed(gain2_grad, 0).reshape(devices, -1),
        ],
        axis=1,
    )
    head_sums = embed(jnp.sum(head_grads, axis=0)[:3, :heads_mine], 1).reshape(1, -1)
    packed = jnp.concatenate([packed, jnp.broadcast_to(head_sums, (devices, 3 * heads))], axis=1)
    fill = -(-packed.shape[1] // 1024) * 1024 - packed.shape[1]
    packed = jnp.pad(packed, ((0, 0), (0, fill))).reshape(devices, -1, LANES)
    packed = sum_blocks(packed, ALL_AXES).reshape(-1)
    at = 0
    small_grads = []
    for shape in (norm_gain.shape, conv_weight.shape, conv_bias.shape, norm2_gain.shape):
        count = 1
        for dim in shape:
            count *= dim
        small_grads.append(packed[at : at + count].reshape(shape))
        at += count
    head_sums = packed[used : used + 3 * heads].reshape(3, heads)

    return (
        block_out,
        tokens_grad,
        small_grads[0],
        main_grad,
        step_grad,
        small_grads[1],
        small_grads[2],
        head_sums[0],
        head_sums[1],
        head_sums[2],
        small_grads[3],
        out_share,
    )


def solution(mesh):
    dp, fsdp = mesh.shape["dp"], mesh.shape["fsdp"]
    counts = (2, dp // 4, fsdp)
    split = Mesh(mesh.devices.reshape(2, dp // 4, 2, fsdp), ALL_AXES)
    in_specs = (
        P(None, ALL_AXES, None, None),
        P(ALL_AXES),
        P(ALL_AXES, None),
        P(ALL_AXES, None),
        P(None, ALL_AXES),
        P(ALL_AXES),
        P(),
        P(),
        P(),
        P(ALL_AXES),
        P(ALL_AXES, None),
        P(None, ALL_AXES, None, None),
    )
    out_specs = (
        P(None, ALL_AXES, None, None),
        P(None, ALL_AXES, None, None),
        P(ALL_AXES),
        P(ALL_AXES, None),
        P(ALL_AXES, None),
        P(None, ALL_AXES),
        P(ALL_AXES),
        P(),
        P(),
        P(),
        P(ALL_AXES),
        P(ALL_AXES, None),
    )

    def layer(*args):
        return on_device(counts, *args)

    return jax.shard_map(
        layer, mesh=split, in_specs=in_specs, out_specs=out_specs, check_vma=False
    )
```
